512 devices in a mesh: blk: 32 (over z, core), ctr: 16 (over x, y).
Axes of the slice: x: 4, y: 4, z: 16, core: 2. Of those that a mesh axis runs over, the one named last changes fastest.
Arguments:
- integrals: float32 [32, 800, 12800], P('blk', None, 'ctr'), may hold values from -0.078125 to 0.078125
- amplitudes: float32 [8, 12800, 128], P(None, 'ctr', 'blk'), may hold values from -6 to 6
- blockmap: int32 [32], replicated, may hold values from 0 to 31, each once
- vir_energy: float32 [320], replicated, may hold values from 0.2 to 3
- occ_energy: float32 [32], replicated, may hold values from -2 to -0.3
Outputs:
- ladder: float32 [32, 800, 128], P('blk', 'ctr')
- increment: float32 [32, 800, 128], P('blk', 'ctr')
The draws below stay inside these ranges and needn't reach their ends.
Inputs may be any that keep to these rules, and one draw needn't show every extreme that they name: `blockmap`: every block number appears in exactly one slot.
All inputs are finite; a program needn't handle non-finite values.
Results may differ from the reference program's by a relative error of at most 0.0003.
Values sent between devices are 32-bit elements; how exact they have to be, the bound alone decides.
A program may use at most 64 MiB of HBM per device.

```python
import jax
import jax.numpy as jnp
from jax import lax

NIRR = 8
VI = 40
OI = 4
NVIR = 320
NOCC = 32
CD = 12800
IJ = 128
QB = 4
AB_BLK = 800
N_BLK = 32


def spiked(array, stream_key, source, target, blocks, factor):
    owner, partner = [(jnp.arange(array.shape[dim]) // (array.shape[dim] // blocks)).reshape([-1 if axis == dim else 1 for axis in range(array.ndim)]) for dim in (source, target)]
    chosen = jax.random.permutation(stream_key, blocks)[partner]
    strong = (owner == chosen) | (owner == (partner + blocks // 2) % blocks)
    return jnp.where(strong, factor * array, array)


def block_scale(key, extent, pieces, least, high):
    gain, own = 1.0, jax.random.fold_in(key, 6)
    for axis_at, parts in pieces:
        steps = jnp.exp(jax.random.uniform(jax.random.fold_in(own, axis_at), (parts,), jnp.float32, least / len(pieces), high / len(pieces)))
        gain = gain * jnp.repeat(steps, extent[axis_at] // parts).reshape([-1 if axis == axis_at else 1 for axis in range(len(extent))])
    return gain


def centred(stream_key, extent, width, reach, split=(), kind=jnp.bfloat16):
    drawn = width * jax.random.normal(stream_key, extent, jnp.float32)
    if split:
        drawn = drawn * block_scale(stream_key, extent, split, -0.22, 0.18)
    return jnp.clip(drawn, -reach, reach).astype(kind)


def noise_with(own_key, extent, deviation, most, cuts, heavy, kind=jnp.bfloat16):
    array = deviation * jax.random.normal(own_key, extent, jnp.float32)
    if cuts:
        array = array * block_scale(own_key, extent, cuts, -0.22, 0.18)
    return jnp.clip(spiked(array, jax.random.fold_in(own_key, 3), *heavy), -most, most).astype(kind)


def setup_inputs(seed: int = 0) -> dict:
    keys = jax.random.split(jax.random.key(seed), 6)
    integrals = noise_with(keys[0], (N_BLK, AB_BLK, CD), CD ** -0.5, 0.078125, ((0, 32), (2, 16)), (2, 1, 16, 2.0), jnp.float32)
    amplitudes = centred(keys[1], (NIRR, CD, IJ), 1.0, 6.0, ((1, 16), (2, 32)), jnp.float32)
    blockmap = jax.random.permutation(keys[2], N_BLK).astype(jnp.int32)
    vir_energy = jnp.clip(jax.random.uniform(keys[3], (NVIR,), jnp.float32, 0.2, 3.0), 0.2, 3.0)
    occ_energy = jnp.clip(jax.random.uniform(keys[4], (NOCC,), jnp.float32, -2.0, -0.3), -2.0, -0.3)
    return dict(integrals=integrals, amplitudes=amplitudes, blockmap=blockmap, vir_energy=vir_energy, occ_energy=occ_energy)


def denominator(block, start, count, vir_energy, occ_energy):
    irrep = block // QB
    rows = (block % QB) * AB_BLK + start + jnp.arange(count, dtype=jnp.int32)
    arow = rows // (VI * VI)
    first = arow * VI + (rows // VI) % VI
    second = jnp.bitwise_xor(arow, irrep) * VI + rows % VI
    cols = jnp.arange(IJ, dtype=jnp.int32)
    orow = cols // (OI * OI)
    hole_one = orow * OI + (cols // OI) % OI
    hole_two = jnp.bitwise_xor(orow, irrep) * OI + cols % OI
    upper = vir_energy[first] + vir_energy[second]
    lower = occ_energy[hole_one] + occ_energy[hole_two]
    return upper[:, None] - lower[None, :]


def reference(integrals, amplitudes, blockmap, vir_energy, occ_energy):
    def single(pair):
        block_ints, block = pair
        amps = amplitudes[block // QB]
        product = jnp.dot(block_ints, amps, preferred_element_type=jnp.float32, precision=lax.Precision.HIGHEST)
        denom = denominator(block, 0, AB_BLK, vir_energy, occ_energy)
        return product, product / denom

    ladder, increment = lax.map(single, (integrals, blockmap))
    return ladder, increment
```

```python
import functools

import jax
import jax.numpy as jnp
from jax import lax
from jax.experimental import pallas as pl
from jax.experimental.pallas import tpu as pltpu
from jax.sharding import PartitionSpec as P

NIRR = 8
VI = 40
OI = 4
MESH = pl.DeviceIdType.MESH
NT = (((1,), (1,)), ((), ()))


def denominator(block, groups, ab_block, start, count, columns, vir, occ_ref):
    irrep = block // groups
    quarter = block - irrep * groups
    rows = quarter * ab_block + start + lax.broadcasted_iota(jnp.int32, (count, 1), 0)
    first = (rows * 52429) >> 21
    digit = rows - first * VI
    arow = (first * 52429) >> 21
    second = jnp.bitwise_xor(arow, irrep) * VI + digit
    index = lax.broadcasted_iota(jnp.int32, (1, vir.shape[1]), 1)
    up_one = jnp.sum(jnp.where(index == first, vir, 0.0), axis=1, keepdims=True)
    up_two = jnp.sum(jnp.where(index == second, vir, 0.0), axis=1, keepdims=True)
    cols = lax.broadcasted_iota(jnp.int32, (1, columns), 1)
    hole_one = cols >> 2
    hole_two = jnp.bitwise_xor(cols >> 4, irrep) * OI + (cols & 3)
    low_one = jnp.zeros((1, columns), jnp.float32)
    low_two = jnp.zeros((1, columns), jnp.float32)
    for o in range(NIRR * OI):
        low_one = jnp.where(hole_one == o, occ_ref[o], low_one)
        low_two = jnp.where(hole_two == o, occ_ref[o], low_two)
    return (up_one + up_two) - (low_one + low_two)


def kernel(
    nb, nc, blockmap_ref, occ_ref, vir_ref, amps_ref, ints_hbm,
    ladder_ref, incr_ref,
    ints_f32, ints_hi, ints_lo, outbox, inbox, gathered, partial_sum, sums_out, sums_in, denom_ref,
    ints_sem, a_send, a_recv, s_send, s_recv,
):
    b = lax.axis_index("blk")
    c = lax.axis_index("ctr")
    groups = nb // NIRR
    ab, cd = ints_f32.shape
    share = ab // nc
    mine = amps_ref.shape[1]
    ints_copy = pltpu.make_async_copy(ints_hbm, ints_f32, ints_sem)
    ints_copy.start()

    barrier = pltpu.get_barrier_semaphore()

    @pl.loop(1, nb)
    def _(k):
        pl.semaphore_signal(barrier, inc=1, device_id=(lax.rem(b + k, nb), c), device_id_type=MESH)

    @pl.loop(1, nc)
    def _(k):
        pl.semaphore_signal(barrier, inc=1, device_id=(b, lax.rem(c + k, nc)), device_id_type=MESH)

    for p in range(nb):
        outbox[p] = amps_ref[blockmap_ref[p] // groups]
    pl.semaphore_wait(barrier, nb - 1 + nc - 1)

    def amps_copy(k):
        to = lax.rem(b + k, nb)
        return pltpu.make_async_remote_copy(
            src_ref=outbox.at[to], dst_ref=inbox.at[b], send_sem=a_send.at[k], recv_sem=a_recv.at[k],
            device_id=(to, c), device_id_type=MESH,
        )

    @pl.loop(0, nb - 1)
    def _(i):
        k = nb // 2 + ((i + 1) // 2) * (2 * (i % 2) - 1)
        amps_copy(k).start()

    inbox[b] = amps_ref[blockmap_ref[b] // groups]
    denom_ref[...] = denominator(
        blockmap_ref[b], groups, ab, c * share, share, nb * mine, vir_ref[...], occ_ref
    )
    ints_copy.wait()
    value = ints_f32[...]
    high = value.astype(jnp.bfloat16)
    ints_hi[...] = high
    ints_lo[...] = (value - high.astype(jnp.float32)).astype(jnp.bfloat16)

    @pl.loop(1, nb)
    def _(k):
        amps_copy(k).wait_recv()

    for p in range(nb):
        gathered[p * mine:(p + 1) * mine, :] = inbox[p]
    amps = gathered[...]
    amps_hi = amps.astype(jnp.bfloat16)
    amps_lo = (amps - amps_hi.astype(jnp.float32)).astype(jnp.bfloat16)
    dot = functools.partial(lax.dot_general, dimension_numbers=NT, preferred_element_type=jnp.float32)
    step = 160
    for r in range(0, ab, step):
        high = ints_hi[r:r + step, :]
        partial_sum[r:r + step, :] = (
            dot(ints_lo[r:r + step, :], amps_hi) + dot(high, amps_lo) + dot(high, amps_hi)
        )
    for p in range(nc):
        sums_out[p] = partial_sum[p * share:(p + 1) * share, :]

    def sums_copy(k):
        to = lax.rem(c + k, nc)
        return pltpu.make_async_remote_copy(
            src_ref=sums_out.at[to], dst_ref=sums_in.at[c], send_sem=s_send.at[k], recv_sem=s_recv.at[k],
            device_id=(b, to), device_id_type=MESH,
        )

    @pl.loop(1, nc)
    def _(k):
        sums_copy(k).start()

    sums_in[c] = sums_out[c]

    @pl.loop(1, nc)
    def _(k):
        sums_copy(k).wait_recv()

    total = sums_in[0]
    for p in range(1, nc):
        total = total + sums_in[p]
    ladder_ref[...] = total
    incr_ref[...] = total / denom_ref[...]

    @pl.loop(1, nb)
    def _(k):
        amps_copy(k).wait_send()

    @pl.loop(1, nc)
    def _(k):
        sums_copy(k).wait_send()


def on_device(integrals, amplitudes, blockmap, vir_energy, occ_energy):
    nb, nc = lax.axis_size("blk"), lax.axis_size("ctr")
    _, ab, cd = integrals.shape
    irreps, _, mine = amplitudes.shape
    ij = mine * nb
    share = ab // nc
    vmem = pl.BlockSpec(memory_space=pltpu.VMEM)
    smem = pl.BlockSpec(memory_space=pltpu.SMEM)
    out = jax.ShapeDtypeStruct((share, ij), jnp.float32)
    ladder, increment = pl.pallas_call(
        functools.partial(kernel, nb, nc),
        out_shape=(out, out),
        in_specs=[smem, smem, vmem, vmem, pl.BlockSpec(memory_space=pl.ANY)],
        out_specs=(vmem, vmem),
        scratch_shapes=[
            pltpu.VMEM((ab, cd), jnp.float32),
            pltpu.VMEM((ab, cd), jnp.bfloat16),
            pltpu.VMEM((ab, cd), jnp.bfloat16),
            pltpu.VMEM((nb, mine, cd), jnp.float32),
            pltpu.VMEM((nb, mine, cd), jnp.float32),
            pltpu.VMEM((ij, cd), jnp.float32),
            pltpu.VMEM((ab, ij), jnp.float32),
            pltpu.VMEM((nc, share, ij), jnp.float32),
            pltpu.VMEM((nc, share, ij), jnp.float32),
            pltpu.VMEM((share, ij), jnp.float32),
            pltpu.SemaphoreType.DMA,
            pltpu.SemaphoreType.DMA((nb,)),
            pltpu.SemaphoreType.DMA((nb,)),
            pltpu.SemaphoreType.DMA((nc,)),
            pltpu.SemaphoreType.DMA((nc,)),
        ],
        compiler_params=pltpu.CompilerParams(
            collective_id=0, has_side_effects=True, vmem_limit_bytes=48 << 20
        ),
    )(
        blockmap, occ_energy, vir_energy[None, :], jnp.transpose(amplitudes, (0, 2, 1)), integrals[0]
    )
    return ladder[None], increment[None]


def solution(mesh):
    placed = (P("blk", None, "ctr"), P(None, "ctr", "blk"), P(), P(), P())
    return jax.shard_map(
        on_device,
        mesh=mesh,
        in_specs=placed,
        out_specs=(P("blk", "ctr", None), P("blk", "ctr", None)),
        check_vma=False,
    )
```

```python
import functools

import jax
import jax.numpy as jnp
from jax import lax
from jax.experimental import pallas as pl
from jax.experimental.pallas import tpu as pltpu
from jax.sharding import PartitionSpec as P

NIRR = 8
VI = 40
OI = 4
MESH = pl.DeviceIdType.MESH
NT = (((1,), (1,)), ((), ()))


def denominator(block, groups, ab_block, start, count, columns, vir, occ_ref):
    irrep = block // groups
    quarter = block - irrep * groups
    rows = quarter * ab_block + start + lax.broadcasted_iota(jnp.int32, (count, 1), 0)
    first = (rows * 52429) >> 21
    digit = rows - first * VI
    arow = (first * 52429) >> 21
    second = jnp.bitwise_xor(arow, irrep) * VI + digit
    index = lax.broadcasted_iota(jnp.int32, (1, vir.shape[1]), 1)
    up_one = jnp.sum(jnp.where(index == first, vir, 0.0), axis=1, keepdims=True)
    up_two = jnp.sum(jnp.where(index == second, vir, 0.0), axis=1, keepdims=True)
    cols = lax.broadcasted_iota(jnp.int32, (1, columns), 1)
    hole_one = cols >> 2
    hole_two = jnp.bitwise_xor(cols >> 4, irrep) * OI + (cols & 3)
    low_one = jnp.zeros((1, columns), jnp.float32)
    low_two = jnp.zeros((1, columns), jnp.float32)
    for o in range(NIRR * OI):
        low_one = jnp.where(hole_one == o, occ_ref[o], low_one)
        low_two = jnp.where(hole_two == o, occ_ref[o], low_two)
    return (up_one + up_two) - (low_one + low_two)


def rank_of(b):
    z, core = b // 2, b % 2
    place = jnp.where(z < 7, z, jnp.where(z < 11, 2 * z - 6, 37 - 2 * z))
    return 2 * place + core


def at_rank(rank):
    place, core = rank // 2, rank % 2
    z = jnp.where(place < 7, place, jnp.where(place % 2 == 1, 15 - (place - 7) // 2, 7 + (place - 8) // 2))
    return 2 * z + core


def kernel(
    nb, nc, blockmap_hbm, occ_hbm, vir_hbm, amps_hbm, ints_hbm,
    ladder_ref, incr_ref,
    blockmap_ref, occ_ref, vir_ref, amps_ref,
    ints_f32, ints_hi, ints_lo, outbox, inbox, gathered, partial_sum, sums_out, sums_in, denom_ref,
    fetch_sem, a_send, a_recv, s_send, s_recv, a_ready, s_ready,
):
    b = lax.axis_index("blk")
    c = lax.axis_index("ctr")
    rank = rank_of(b)
    groups = nb // NIRR
    ab, cd = ints_f32.shape
    share = ab // nc
    mine = amps_ref.shape[1]
    fetches = [
        pltpu.make_async_copy(src, dst, fetch_sem.at[i])
        for i, (src, dst) in enumerate(
            [(blockmap_hbm, blockmap_ref), (amps_hbm, amps_ref), (occ_hbm, occ_ref), (vir_hbm, vir_ref.at[0]),
             (ints_hbm, ints_f32)]
        )
    ]
    for fetch in fetches:
        fetch.start()

    barrier = pltpu.get_barrier_semaphore()

    @pl.loop(rank + 1, nb)
    def _(r):
        pl.semaphore_signal(barrier, inc=1, device_id=(at_rank(r), c), device_id_type=MESH)

    @pl.loop(c + 1, nc)
    def _(p):
        pl.semaphore_signal(barrier, inc=1, device_id=(b, p), device_id_type=MESH)

    @pl.when(rank + c > 0)
    def _():
        pl.semaphore_wait(barrier, rank + c)

    @pl.loop(0, rank)
    def _(r):
        pl.semaphore_signal(a_ready.at[b], inc=1, device_id=(at_rank(r), c), device_id_type=MESH)

    @pl.loop(0, c)
    def _(p):
        pl.semaphore_signal(s_ready, inc=1, device_id=(b, p), device_id_type=MESH)

    def amps_copy(to):
        return pltpu.make_async_remote_copy(
            src_ref=outbox.at[to], dst_ref=inbox.at[b], send_sem=a_send.at[to], recv_sem=a_recv.at[b],
            device_id=(to, c), device_id_type=MESH,
        )

    def amps_arrival(p):
        return pltpu.make_async_remote_copy(
            src_ref=outbox.at[p], dst_ref=inbox.at[p], send_sem=a_send.at[p], recv_sem=a_recv.at[p],
            device_id=(p, c), device_id_type=MESH,
        )

    fetches[0].wait()
    fetches[1].wait()

    def send_amps(to):
        outbox[to] = amps_ref[blockmap_ref[to] // groups]
        amps_copy(to).start()

    @pl.loop(0, rank)
    def _(r):
        send_amps(at_rank(r))

    @pl.loop(rank + 1, nb)
    def _(r):
        to = at_rank(r)
        pl.semaphore_wait(a_ready.at[to], 1)
        send_amps(to)

    inbox[b] = amps_ref[blockmap_ref[b] // groups]
    fetches[2].wait()
    fetches[3].wait()
    denom_ref[...] = denominator(
        blockmap_ref[b], groups, ab, c * share, share, nb * mine, vir_ref[...], occ_ref
    )
    fetches[4].wait()
    value = ints_f32[...]
    high = value.astype(jnp.bfloat16)
    ints_hi[...] = high
    ints_lo[...] = (value - high.astype(jnp.float32)).astype(jnp.bfloat16)

    @pl.loop(0, nb)
    def _(p):
        @pl.when(p != b)
        def _():
            amps_arrival(p).wait_recv()

    for p in range(nb):
        gathered[p * mine:(p + 1) * mine, :] = inbox[p]
    amps = gathered[...]
    amps_hi = amps.astype(jnp.bfloat16)
    amps_lo = (amps - amps_hi.astype(jnp.float32)).astype(jnp.bfloat16)
    dot = functools.partial(lax.dot_general, dimension_numbers=NT, preferred_element_type=jnp.float32)
    step = 160
    for r in range(0, ab, step):
        high = ints_hi[r:r + step, :]
        partial_sum[r:r + step, :] = (
            dot(ints_lo[r:r + step, :], amps_hi) + dot(high, amps_lo) + dot(high, amps_hi)
        )
    for p in range(nc):
        sums_out[p] = partial_sum[p * share:(p + 1) * share, :]

    def sums_copy(k):
        to = lax.rem(c + k, nc)
        return pltpu.make_async_remote_copy(
            src_ref=sums_out.at[to], dst_ref=sums_in.at[c], send_sem=s_send.at[k], recv_sem=s_recv.at[k],
            device_id=(b, to), device_id_type=MESH,
        )

    @pl.when(c < nc - 1)
    def _():
        pl.semaphore_wait(s_ready, nc - 1 - c)

    @pl.loop(1, nc)
    def _(k):
        sums_copy(k).start()

    sums_in[c] = sums_out[c]

    @pl.loop(1, nc)
    def _(k):
        sums_copy(k).wait_recv()

    total = sums_in[0]
    for p in range(1, nc):
        total = total + sums_in[p]
    ladder_ref[:, 0, :] = total
    incr_ref[:, 0, :] = total / denom_ref[...]

    @pl.loop(0, nb)
    def _(p):
        @pl.when(p != b)
        def _():
            amps_copy(p).wait_send()

    @pl.loop(1, nc)
    def _(k):
        sums_copy(k).wait_send()


def on_device(integrals, amplitudes, blockmap, vir_energy, occ_energy):
    nb, nc = lax.axis_size("blk"), lax.axis_size("ctr")
    _, ab, cd = integrals.shape
    irreps, _, mine = amplitudes.shape
    ij = mine * nb
    share = ab // nc
    vmem = pl.BlockSpec(memory_space=pltpu.VMEM)
    hbm = pl.BlockSpec(memory_space=pl.ANY)
    out = jax.ShapeDtypeStruct((share, 1, ij), jnp.float32)
    ladder, increment = pl.pallas_call(
        functools.partial(kernel, nb, nc),
        out_shape=(out, out),
        in_specs=[hbm] * 5,
        out_specs=(vmem, vmem),
        scratch_shapes=[
            pltpu.SMEM(blockmap.shape, jnp.int32),
            pltpu.SMEM(occ_energy.shape, jnp.float32),
            pltpu.VMEM((1, vir_energy.shape[0]), jnp.float32),
            pltpu.VMEM((irreps, mine, cd), jnp.float32),
            pltpu.VMEM((ab, cd), jnp.float32),
            pltpu.VMEM((ab, cd), jnp.bfloat16),
            pltpu.VMEM((ab, cd), jnp.bfloat16),
            pltpu.VMEM((nb, mine, cd), jnp.float32),
            pltpu.VMEM((nb, mine, cd), jnp.float32),
            pltpu.VMEM((ij, cd), jnp.float32),
            pltpu.VMEM((ab, ij), jnp.float32),
            pltpu.VMEM((nc, share, ij), jnp.float32),
            pltpu.VMEM((nc, share, ij), jnp.float32),
            pltpu.VMEM((share, ij), jnp.float32),
            pltpu.SemaphoreType.DMA((5,)),
            pltpu.SemaphoreType.DMA((nb,)),
            pltpu.SemaphoreType.DMA((nb,)),
            pltpu.SemaphoreType.DMA((nc,)),
            pltpu.SemaphoreType.DMA((nc,)),
            pltpu.SemaphoreType.REGULAR((nb,)),
            pltpu.SemaphoreType.REGULAR,
        ],
        compiler_params=pltpu.CompilerParams(
            collective_id=0, has_side_effects=True, vmem_limit_bytes=60 << 20
        ),
    )(
        blockmap, occ_energy, vir_energy, jnp.transpose(amplitudes, (0, 2, 1)), integrals[0]
    )
    return jnp.transpose(ladder, (1, 0, 2)), jnp.transpose(increment, (1, 0, 2))


def solution(mesh):
    placed = (P("blk", None, "ctr"), P(None, "ctr", "blk"), P(), P(), P())
    return jax.shard_map(
        on_device,
        mesh=mesh,
        in_specs=placed,
        out_specs=(P("blk", "ctr", None), P("blk", "ctr", None)),
        check_vma=False,
    )
```

```python
import functools

import jax
import jax.numpy as jnp
from jax import lax
from jax.experimental import pallas as pl
from jax.experimental.pallas import tpu as pltpu
from jax.sharding import PartitionSpec as P

NIRR = 8
VI = 40
OI = 4
LANES = 128
MESH = pl.DeviceIdType.MESH
CHUNKS = 2
VLIM = 52 << 20
NT = (((1,), (1,)), ((), ()))


def denominator(block, groups, ab_block, start, count, columns, vir, occ_ref):
    irrep = block >> 2
    quarter = block - irrep * groups
    rows = quarter * ab_block + start + lax.broadcasted_iota(jnp.int32, (count, 1), 0)
    first = (rows * 52429) >> 21
    digit = rows - first * VI
    arow = (first * 52429) >> 21
    second = jnp.bitwise_xor(arow, irrep) * VI + digit
    index = lax.broadcasted_iota(jnp.int32, (1, vir.shape[1]), 1)
    up_one = jnp.sum(jnp.where(index == first, vir, 0.0), axis=1, keepdims=True)
    up_two = jnp.sum(jnp.where(index == second, vir, 0.0), axis=1, keepdims=True)
    cols = lax.broadcasted_iota(jnp.int32, (1, columns), 1)
    hole_one = cols >> 2
    hole_two = jnp.bitwise_xor(cols >> 4, irrep) * OI + (cols & 3)
    low_one = jnp.zeros((1, columns), jnp.float32)
    low_two = jnp.zeros((1, columns), jnp.float32)
    for o in range(NIRR * OI):
        low_one = jnp.where(hole_one == o, occ_ref[o], low_one)
        low_two = jnp.where(hole_two == o, occ_ref[o], low_two)
    return (up_one + up_two) - (low_one + low_two)


def rank_of(b):
    z = b >> 1
    return 2 * jnp.where(z < 7, z, jnp.where(z < 11, 2 * z - 6, 37 - 2 * z)) + (b & 1)


def at_rank(rank):
    place = rank >> 1
    half = (place - 7) >> 1
    z = jnp.where(place < 7, place, jnp.where((place & 1) == 1, 15 - half, 7 + half))
    return 2 * z + (rank & 1)


def kernel(
    nb, nc, blockmap_hbm, occ_hbm, vir_hbm, amps_hbm, ints_hbm,
    ladder_ref, incr_ref,
    blockmap_ref, occ_ref, vir_ref, amps_ref,
    ints_f32, ints_hi, ints_lo, packed, outbox, inbox, gathered, product, sums_out, sums_in,
    totals, denom_ref, fetch_sem, a_send, a_recv, s_send, s_recv, a_ready, s_ready,
):
    b = lax.axis_index("blk")
    c = lax.axis_index("ctr")
    rank = rank_of(b)
    early = 14
    groups = nb // NIRR
    ab, cd = ints_f32.shape
    share = ab // nc
    irreps, mine, _ = amps_ref.shape
    full = cd // LANES
    rest = cd - full * LANES
    ij = nb * mine
    width = ij // CHUNKS
    height = sums_out.shape[2]
    starts = [min(g * height, share - height) for g in range(CHUNKS)]
    fetches = [
        pltpu.make_async_copy(src, dst, fetch_sem.at[i])
        for i, (src, dst) in enumerate(
            [(blockmap_hbm, blockmap_ref), (amps_hbm, amps_ref), (occ_hbm, occ_ref), (vir_hbm, vir_ref.at[0]),
             (ints_hbm, ints_f32)]
        )
    ]
    for fetch in fetches:
        fetch.start()

    barrier = pltpu.get_barrier_semaphore()

    @pl.loop(rank + 1, nb)
    def _(r):
        pl.semaphore_signal(barrier, inc=1, device_id=(at_rank(r), c), device_id_type=MESH)

    @pl.loop(c + 1, nc)
    def _(p):
        pl.semaphore_signal(barrier, inc=1, device_id=(b, p), device_id_type=MESH)

    @pl.when(rank + c > 0)
    def _():
        pl.semaphore_wait(barrier, rank + c)

    @pl.loop(0, rank)
    def _(r):
        pl.semaphore_signal(a_ready.at[b], inc=1, device_id=(at_rank(r), c), device_id_type=MESH)

    @pl.loop(0, c)
    def _(p):
        pl.semaphore_signal(s_ready, inc=1, device_id=(b, p), device_id_type=MESH)

    fetches[0].wait()
    fetches[1].wait()
    for h in range(irreps):
        for t in range(full):
            packed[h, t * mine:(t + 1) * mine, :] = amps_ref[h, :, t * LANES:(t + 1) * LANES]
        packed[h, full * mine:full * mine + 1, :] = jnp.concatenate(
            [amps_ref[h, u:u + 1, full * LANES:cd] for u in range(mine)], axis=1
        )

    def amps_copy(to):
        return pltpu.make_async_remote_copy(
            src_ref=outbox.at[to], dst_ref=inbox.at[b], send_sem=a_send.at[to], recv_sem=a_recv.at[b],
            device_id=(to, c), device_id_type=MESH,
        )

    def amps_arrival(p):
        return pltpu.make_async_remote_copy(
            src_ref=outbox.at[p], dst_ref=inbox.at[p], send_sem=a_send.at[p], recv_sem=a_recv.at[p],
            device_id=(p, c), device_id_type=MESH,
        )

    def visit(to):
        @pl.when(rank_of(to) > rank)
        def _():
            pl.semaphore_wait(a_ready.at[to], 1)

        outbox[to] = packed[blockmap_ref[to] >> 2]
        amps_copy(to).start()

    def far(i):
        return (b + nb // 2 + ((i + 1) >> 1) * (2 * (i & 1) - 1)) & (nb - 1)

    @pl.when(rank < early)
    def _():
        @pl.loop(0, early)
        def _(r):
            @pl.when(r != rank)
            def _():
                visit(at_rank(r))

    @pl.when(rank >= early)
    def _():
        @pl.loop(0, nb - 1)
        def _(i):
            to = far(i)

            @pl.when(rank_of(to) < early)
            def _():
                visit(to)

    @pl.loop(0, nb - 1)
    def _(i):
        to = far(i)

        @pl.when(rank_of(to) >= early)
        def _():
            visit(to)

    inbox[b] = packed[blockmap_ref[b] >> 2]
    fetches[2].wait()
    fetches[3].wait()
    denom_ref[...] = denominator(
        blockmap_ref[b], groups, ab, c * share, share, ij, vir_ref[...], occ_ref
    )
    fetches[4].wait()
    value = ints_f32[...]
    high = value.astype(jnp.bfloat16)
    ints_hi[...] = high
    ints_lo[...] = (value - high.astype(jnp.float32)).astype(jnp.bfloat16)

    def sums_copy(j, to):
        return pltpu.make_async_remote_copy(
            src_ref=sums_out.at[j, to], dst_ref=sums_in.at[j, c],
            send_sem=s_send.at[j * nc + to], recv_sem=s_recv.at[j * nc + c],
            device_id=(b, to), device_id_type=MESH,
        )

    def sums_arrival(j, p):
        return pltpu.make_async_remote_copy(
            src_ref=sums_out.at[j, p], dst_ref=sums_in.at[j, p],
            send_sem=s_send.at[j * nc + p], recv_sem=s_recv.at[j * nc + p],
            device_id=(b, p), device_id_type=MESH,
        )

    lane = lax.broadcasted_iota(jnp.int32, (height, ij), 1)
    dot = functools.partial(lax.dot_general, dimension_numbers=NT, preferred_element_type=jnp.float32)
    sources = nb // CHUNKS

    def multiply(j):
        base = j * sources

        @pl.loop(base, base + sources)
        def _(p):
            @pl.when(p != b)
            def _():
                amps_arrival(p).wait_recv()

        for p in range(sources):
            for t in range(full):
                gathered[p * mine:(p + 1) * mine, t * LANES:(t + 1) * LANES] = (
                    inbox[base + p, t * mine:(t + 1) * mine, :]
                )
            row = inbox[base + p, full * mine:full * mine + 1, :]
            for u in range(mine):
                gathered[p * mine + u:p * mine + u + 1, full * LANES:cd] = row[:, u * rest:(u + 1) * rest]
        amps = gathered[...]
        amps_hi = amps.astype(jnp.bfloat16)
        amps_lo = (amps - amps_hi.astype(jnp.float32)).astype(jnp.bfloat16)
        both = jnp.concatenate([amps_hi] * CHUNKS + [amps_lo] * CHUNKS, axis=0)
        step = 160
        for r in range(0, ab, step):
            wide = dot(ints_hi[r:r + step, :], both)
            product[r:r + step, :] = (
                (dot(ints_lo[r:r + step, :], both[:ij]) + wide[:, ij:]) + wide[:, :ij]
            )
        for p in range(nc):
            rows = [product[p * share + start:p * share + start + height, :] for start in starts]
            block = rows[-1]
            for g in range(CHUNKS - 2, -1, -1):
                block = jnp.where(lane < (g + 1) * width, rows[g], block)
            sums_out[j, p] = block

        @pl.loop(1, nc)
        def _(k):
            sums_copy(j, (c + k) & (nc - 1)).start()

        sums_in[j, c] = sums_out[j, c]

    def add_up(j):
        @pl.loop(0, nc)
        def _(p):
            @pl.when(p != c)
            def _():
                sums_arrival(j, p).wait_recv()

        total = sums_in[j, 0]
        for p in range(1, nc):
            total = total + sums_in[j, p]
        totals[j] = total

    order = [0, 1, 3, 2] if CHUNKS == 4 else list(range(CHUNKS))
    for place, j in enumerate(order):
        multiply_at = j
        if place == 0:
            @pl.when(c < nc - 1)
            def _():
                pl.semaphore_wait(s_ready, nc - 1 - c)
        multiply(multiply_at)
    for j in order:
        add_up(j)

    for g, start in enumerate(starts):
        block = None
        for j in range(CHUNKS):
            turned = totals[j]
            if (j - g) % CHUNKS:
                turned = pltpu.roll(turned, (j - g) % CHUNKS * width, 1)
            block = turned if block is None else jnp.where(lane < j * width, block, turned)
        ladder_ref[start:start + height, 0, :] = block
        incr_ref[start:start + height, 0, :] = block / denom_ref[start:start + height, :]

    @pl.loop(0, nb)
    def _(p):
        @pl.when(p != b)
        def _():
            amps_copy(p).wait_send()

    for j in range(CHUNKS):
        @pl.loop(0, nc)
        def _(p):
            @pl.when(p != c)
            def _():
                sums_copy(j, p).wait_send()


def on_device(integrals, amplitudes, blockmap, vir_energy, occ_energy):
    nb, nc = lax.axis_size("blk"), lax.axis_size("ctr")
    _, ab, cd = integrals.shape
    irreps, _, mine = amplitudes.shape
    ij = mine * nb
    share = ab // nc
    height = -(-share // CHUNKS)
    rows = mine * cd // LANES
    vmem = pl.BlockSpec(memory_space=pltpu.VMEM)
    hbm = pl.BlockSpec(memory_space=pltpu.HBM)
    out = jax.ShapeDtypeStruct((share, 1, ij), jnp.float32)
    ladder, increment = pl.pallas_call(
        functools.partial(kernel, nb, nc),
        out_shape=(out, out),
        in_specs=[hbm] * 5,
        out_specs=(vmem, vmem),
        scratch_shapes=[
            pltpu.SMEM(blockmap.shape, jnp.int32),
            pltpu.SMEM(occ_energy.shape, jnp.float32),
            pltpu.VMEM((1, vir_energy.shape[0]), jnp.float32),
            pltpu.VMEM((irreps, mine, cd), jnp.float32),
            pltpu.VMEM((ab, cd), jnp.float32),
            pltpu.VMEM((ab, cd), jnp.bfloat16),
            pltpu.VMEM((ab, cd), jnp.bfloat16),
            pltpu.VMEM((irreps, rows, LANES), jnp.float32),
            pltpu.VMEM((nb, rows, LANES), jnp.float32),
            pltpu.VMEM((nb, rows, LANES), jnp.float32),
            pltpu.VMEM((ij // CHUNKS, cd), jnp.float32),
            pltpu.VMEM((ab, ij), jnp.float32),
            pltpu.VMEM((CHUNKS, nc, height, ij), jnp.float32),
            pltpu.VMEM((CHUNKS, nc, height, ij), jnp.float32),
            pltpu.VMEM((CHUNKS, height, ij), jnp.float32),
            pltpu.VMEM((share, ij), jnp.float32),
            pltpu.SemaphoreType.DMA((5,)),
            pltpu.SemaphoreType.DMA((nb,)),
            pltpu.SemaphoreType.DMA((nb,)),
            pltpu.SemaphoreType.DMA((CHUNKS * nc,)),
            pltpu.SemaphoreType.DMA((CHUNKS * nc,)),
            pltpu.SemaphoreType.REGULAR((nb,)),
            pltpu.SemaphoreType.REGULAR,
        ],
        compiler_params=pltpu.CompilerParams(
            collective_id=0, has_side_effects=True, vmem_limit_bytes=VLIM
        ),
    )(
        *(
            pltpu.with_memory_space_constraint(x, pltpu.HBM)
            for x in (blockmap, occ_energy, vir_energy, jnp.transpose(amplitudes, (0, 2, 1)), integrals[0])
        )
    )
    return jnp.transpose(ladder, (1, 0, 2)), jnp.transpose(increment, (1, 0, 2))


def solution(mesh):
    placed = (P("blk", None, "ctr"), P(None, "ctr", "blk"), P(), P(), P())
    return jax.shard_map(
        on_device,
        mesh=mesh,
        in_specs=placed,
        out_specs=(P("blk", "ctr", None), P("blk", "ctr", None)),
        check_vma=False,
    )
```

```python
import functools

import jax
import jax.numpy as jnp
from jax import lax
from jax.experimental import pallas as pl
from jax.experimental.pallas import tpu as pltpu
from jax.sharding import PartitionSpec as P

NIRR = 8
VI = 40
OI = 4
LANES = 128
MESH = pl.DeviceIdType.MESH
CHUNKS = 2
VLIM = 52 << 20
NT = (((1,), (1,)), ((), ()))


def denominator(block, groups, ab_block, start, count, columns, vir, occ_ref):
    irrep = block >> 2
    quarter = block - irrep * groups
    rows = quarter * ab_block + start + lax.broadcasted_iota(jnp.int32, (count, 1), 0)
    first = (rows * 52429) >> 21
    digit = rows - first * VI
    arow = (first * 52429) >> 21
    second = jnp.bitwise_xor(arow, irrep) * VI + digit
    index = lax.broadcasted_iota(jnp.int32, (1, vir.shape[1]), 1)
    up_one = jnp.sum(jnp.where(index == first, vir, 0.0), axis=1, keepdims=True)
    up_two = jnp.sum(jnp.where(index == second, vir, 0.0), axis=1, keepdims=True)
    cols = lax.broadcasted_iota(jnp.int32, (1, columns), 1)
    hole_one = cols >> 2
    hole_two = jnp.bitwise_xor(cols >> 4, irrep) * OI + (cols & 3)
    low_one = jnp.zeros((1, columns), jnp.float32)
    low_two = jnp.zeros((1, columns), jnp.float32)
    for o in range(NIRR * OI):
        low_one = jnp.where(hole_one == o, occ_ref[o], low_one)
        low_two = jnp.where(hole_two == o, occ_ref[o], low_two)
    return (up_one + up_two) - (low_one + low_two)


def rank_of(b):
    z = b >> 1
    return 2 * jnp.where(z < 7, z, jnp.where(z < 11, 2 * z - 6, 37 - 2 * z)) + (b & 1)


def at_rank(rank):
    place = rank >> 1
    half = (place - 7) >> 1
    z = jnp.where(place < 7, place, jnp.where((place & 1) == 1, 15 - half, 7 + half))
    return 2 * z + (rank & 1)


def kernel(
    nb, nc, blockmap_hbm, occ_hbm, vir_hbm, amps_hbm, ints_hbm,
    ladder_ref, incr_ref,
    blockmap_ref, occ_ref, vir_ref, amps_ref,
    ints_f32, ints_hi, ints_lo, packed, outbox, inbox, gathered, product, sums_out, sums_in,
    totals, denom_ref, fetch_sem, a_send, a_recv, s_send, s_recv, a_ready, s_ready,
):
    b = lax.axis_index("blk")
    c = lax.axis_index("ctr")
    rank = rank_of(b)
    early = 14
    groups = nb // NIRR
    sources = nb // CHUNKS
    ab, cd = ints_f32.shape
    share = ab // nc
    irreps, mine, _ = amps_ref.shape
    full = cd // LANES
    rest = cd - full * LANES
    ij = nb * mine
    width = ij // CHUNKS
    height = sums_out.shape[2]
    starts = [min(g * height, share - height) for g in range(CHUNKS)]
    fetches = [
        pltpu.make_async_copy(src, dst, fetch_sem.at[i])
        for i, (src, dst) in enumerate(
            [(blockmap_hbm, blockmap_ref), (amps_hbm, amps_ref), (occ_hbm, occ_ref), (vir_hbm, vir_ref.at[0]),
             (ints_hbm, ints_f32)]
        )
    ]
    for fetch in fetches:
        fetch.start()

    barrier = pltpu.get_barrier_semaphore()

    @pl.loop(rank + 1, nb)
    def _(r):
        pl.semaphore_signal(barrier, inc=1, device_id=(at_rank(r), c), device_id_type=MESH)

    @pl.loop(c + 1, nc)
    def _(p):
        pl.semaphore_signal(barrier, inc=1, device_id=(b, p), device_id_type=MESH)

    @pl.when(rank + c > 0)
    def _():
        pl.semaphore_wait(barrier, rank + c)

    @pl.loop(0, rank)
    def _(r):
        pl.semaphore_signal(a_ready.at[b], inc=1, device_id=(at_rank(r), c), device_id_type=MESH)

    @pl.loop(0, c)
    def _(p):
        pl.semaphore_signal(s_ready, inc=1, device_id=(b, p), device_id_type=MESH)

    fetches[0].wait()
    fetches[1].wait()
    for h in range(irreps):
        for t in range(full):
            packed[h, t * mine:(t + 1) * mine, :] = amps_ref[h, :, t * LANES:(t + 1) * LANES]
        packed[h, full * mine:full * mine + 1, :] = jnp.concatenate(
            [amps_ref[h, u:u + 1, full * LANES:cd] for u in range(mine)], axis=1
        )

    def amps_copy(to):
        return pltpu.make_async_remote_copy(
            src_ref=outbox.at[to], dst_ref=inbox.at[b], send_sem=a_send, recv_sem=a_recv.at[b // sources],
            device_id=(to, c), device_id_type=MESH,
        )

    def visit(to):
        @pl.when(rank_of(to) > rank)
        def _():
            pl.semaphore_wait(a_ready.at[to], 1)

        outbox[to] = packed[blockmap_ref[to] >> 2]
        amps_copy(to).start()

    def far(i):
        return (b + nb // 2 + ((i + 1) >> 1) * (2 * (i & 1) - 1)) & (nb - 1)

    @pl.when(rank < early)
    def _():
        @pl.loop(0, early)
        def _(r):
            @pl.when(r != rank)
            def _():
                visit(at_rank(r))

    @pl.when(rank >= early)
    def _():
        @pl.loop(0, nb - 1)
        def _(i):
            to = far(i)

            @pl.when(rank_of(to) < early)
            def _():
                visit(to)

    @pl.loop(0, nb - 1)
    def _(i):
        to = far(i)

        @pl.when(rank_of(to) >= early)
        def _():
            visit(to)

    outbox[b] = packed[blockmap_ref[b] >> 2]
    pltpu.make_async_copy(outbox.at[b], inbox.at[b], a_recv.at[b // sources]).start()
    fetches[2].wait()
    fetches[3].wait()
    denom_ref[...] = denominator(
        blockmap_ref[b], groups, ab, c * share, share, ij, vir_ref[...], occ_ref
    )
    fetches[4].wait()
    value = ints_f32[...]
    high = value.astype(jnp.bfloat16)
    ints_hi[...] = high
    ints_lo[...] = (value - high.astype(jnp.float32)).astype(jnp.bfloat16)

    def sums_copy(j, to):
        return pltpu.make_async_remote_copy(
            src_ref=sums_out.at[j, to], dst_ref=sums_in.at[j, c],
            send_sem=s_send.at[j], recv_sem=s_recv.at[j],
            device_id=(b, to), device_id_type=MESH,
        )

    lane = lax.broadcasted_iota(jnp.int32, (height, ij), 1)
    dot = functools.partial(lax.dot_general, dimension_numbers=NT, preferred_element_type=jnp.float32)

    def multiply(j):
        base = j * sources

        arrived = inbox.at[pl.ds(base, sources)]
        pltpu.make_async_copy(arrived, arrived, a_recv.at[j]).wait()

        for p in range(sources):
            for t in range(full):
                gathered[p * mine:(p + 1) * mine, t * LANES:(t + 1) * LANES] = (
                    inbox[base + p, t * mine:(t + 1) * mine, :]
                )
            row = inbox[base + p, full * mine:full * mine + 1, :]
            for u in range(mine):
                gathered[p * mine + u:p * mine + u + 1, full * LANES:cd] = row[:, u * rest:(u + 1) * rest]
        amps = gathered[...]
        amps_hi = amps.astype(jnp.bfloat16)
        amps_lo = (amps - amps_hi.astype(jnp.float32)).astype(jnp.bfloat16)
        both = jnp.concatenate([amps_hi] * CHUNKS + [amps_lo] * CHUNKS, axis=0)
        step = 160
        for r in range(0, ab, step):
            wide = dot(ints_hi[r:r + step, :], both)
            product[r:r + step, :] = (
                (dot(ints_lo[r:r + step, :], both[:ij]) + wide[:, ij:]) + wide[:, :ij]
            )
        for p in range(nc):
            rows = [product[p * share + start:p * share + start + height, :] for start in starts]
            block = rows[-1]
            for g in range(CHUNKS - 2, -1, -1):
                block = jnp.where(lane < (g + 1) * width, rows[g], block)
            sums_out[j, p] = block

        @pl.loop(1, nc)
        def _(k):
            sums_copy(j, (c + k) & (nc - 1)).start()

        pltpu.make_async_copy(sums_out.at[j, c], sums_in.at[j, c], s_recv.at[j]).start()

    def add_up(j):
        pltpu.make_async_copy(sums_in.at[j], sums_in.at[j], s_recv.at[j]).wait()
        total = sums_in[j, 0]
        for p in range(1, nc):
            total = total + sums_in[j, p]
        totals[j] = total

    order = [0, 1, 3, 2] if CHUNKS == 4 else list(range(CHUNKS))
    for place, j in enumerate(order):
        multiply_at = j
        if place == 0:
            @pl.when(c < nc - 1)
            def _():
                pl.semaphore_wait(s_ready, nc - 1 - c)
        multiply(multiply_at)
    sent = outbox.at[pl.ds(0, nb - 1)]
    pltpu.make_async_copy(sent, sent, a_send).wait()
    for j in order:
        sent = sums_out.at[j, pl.ds(0, nc - 1)]
        pltpu.make_async_copy(sent, sent, s_send.at[j]).wait()
    for j in order:
        add_up(j)

    for g, start in enumerate(starts):
        block = None
        for j in range(CHUNKS):
            turned = totals[j]
            if (j - g) % CHUNKS:
                turned = pltpu.roll(turned, (j - g) % CHUNKS * width, 1)
            block = turned if block is None else jnp.where(lane < j * width, block, turned)
        ladder_ref[start:start + height, 0, :] = block
        incr_ref[start:start + height, 0, :] = block / denom_ref[start:start + height, :]


def on_device(integrals, amplitudes, blockmap, vir_energy, occ_energy):
    nb, nc = lax.axis_size("blk"), lax.axis_size("ctr")
    _, ab, cd = integrals.shape
    irreps, _, mine = amplitudes.shape
    ij = mine * nb
    share = ab // nc
    height = -(-share // CHUNKS)
    rows = mine * cd // LANES
    vmem = pl.BlockSpec(memory_space=pltpu.VMEM)
    hbm = pl.BlockSpec(memory_space=pltpu.HBM)
    out = jax.ShapeDtypeStruct((share, 1, ij), jnp.float32)
    ladder, increment = pl.pallas_call(
        functools.partial(kernel, nb, nc),
        out_shape=(out, out),
        in_specs=[hbm] * 5,
        out_specs=(vmem, vmem),
        scratch_shapes=[
            pltpu.SMEM(blockmap.shape, jnp.int32),
            pltpu.SMEM(occ_energy.shape, jnp.float32),
            pltpu.VMEM((1, vir_energy.shape[0]), jnp.float32),
            pltpu.VMEM((irreps, mine, cd), jnp.float32),
            pltpu.VMEM((ab, cd), jnp.float32),
            pltpu.VMEM((ab, cd), jnp.bfloat16),
            pltpu.VMEM((ab, cd), jnp.bfloat16),
            pltpu.VMEM((irreps, rows, LANES), jnp.float32),
            pltpu.VMEM((nb, rows, LANES), jnp.float32),
            pltpu.VMEM((nb, rows, LANES), jnp.float32),
            pltpu.VMEM((ij // CHUNKS, cd), jnp.float32),
            pltpu.VMEM((ab, ij), jnp.float32),
            pltpu.VMEM((CHUNKS, nc, height, ij), jnp.float32),
            pltpu.VMEM((CHUNKS, nc, height, ij), jnp.float32),
            pltpu.VMEM((CHUNKS, height, ij), jnp.float32),
            pltpu.VMEM((share, ij), jnp.float32),
            pltpu.SemaphoreType.DMA((5,)),
            pltpu.SemaphoreType.DMA,
            pltpu.SemaphoreType.DMA((CHUNKS,)),
            pltpu.SemaphoreType.DMA((CHUNKS,)),
            pltpu.SemaphoreType.DMA((CHUNKS,)),
            pltpu.SemaphoreType.REGULAR((nb,)),
            pltpu.SemaphoreType.REGULAR,
        ],
        compiler_params=pltpu.CompilerParams(
            collective_id=0, has_side_effects=True, vmem_limit_bytes=VLIM
        ),
    )(
        *(
            pltpu.with_memory_space_constraint(x, pltpu.HBM)
            for x in (blockmap, occ_energy, vir_energy, jnp.transpose(amplitudes, (0, 2, 1)), integrals[0])
        )
    )
    return jnp.transpose(ladder, (1, 0, 2)), jnp.transpose(increment, (1, 0, 2))


def solution(mesh):
    placed = (P("blk", None, "ctr"), P(None, "ctr", "blk"), P(), P(), P())
    return jax.shard_map(
        on_device,
        mesh=mesh,
        in_specs=placed,
        out_specs=(P("blk", "ctr", None), P("blk", "ctr", None)),
        check_vma=False,
    )
```

```python
import functools

import jax
import jax.numpy as jnp
from jax import lax
from jax.experimental import pallas as pl
from jax.experimental.pallas import tpu as pltpu
from jax.sharding import PartitionSpec as P

NIRR = 8
VI = 40
OI = 4
LANES = 128
MESH = pl.DeviceIdType.MESH
CHUNKS = 2
VLIM = 52 << 20
NT = (((1,), (1,)), ((), ()))


def denominator(block, groups, ab_block, start, count, columns, vir, occ_ref):
    irrep = block >> 2
    quarter = block - irrep * groups
    rows = quarter * ab_block + start + lax.broadcasted_iota(jnp.int32, (count, 1), 0)
    first = (rows * 52429) >> 21
    digit = rows - first * VI
    arow = (first * 52429) >> 21
    second = jnp.bitwise_xor(arow, irrep) * VI + digit
    index = lax.broadcasted_iota(jnp.int32, (1, vir.shape[1]), 1)
    up_one = jnp.sum(jnp.where(index == first, vir, 0.0), axis=1, keepdims=True)
    up_two = jnp.sum(jnp.where(index == second, vir, 0.0), axis=1, keepdims=True)
    cols = lax.broadcasted_iota(jnp.int32, (1, columns), 1)
    hole_one = cols >> 2
    hole_two = jnp.bitwise_xor(cols >> 4, irrep) * OI + (cols & 3)
    low_one = jnp.zeros((1, columns), jnp.float32)
    low_two = jnp.zeros((1, columns), jnp.float32)
    for o in range(NIRR * OI):
        low_one = jnp.where(hole_one == o, occ_ref[o], low_one)
        low_two = jnp.where(hole_two == o, occ_ref[o], low_two)
    return (up_one + up_two) - (low_one + low_two)


def rank_of(b):
    z = b >> 1
    return 2 * jnp.where(z < 7, z, jnp.where(z < 11, 2 * z - 6, 37 - 2 * z)) + (b & 1)


def at_rank(rank):
    place = rank >> 1
    half = (place - 7) >> 1
    z = jnp.where(place < 7, place, jnp.where((place & 1) == 1, 15 - half, 7 + half))
    return 2 * z + (rank & 1)


def kernel(
    nb, nc, blockmap_hbm, occ_hbm, vir_hbm, amps_hbm, ints_hbm,
    ladder_ref, incr_ref,
    blockmap_ref, occ_ref, vir_ref, amps_ref,
    ints_f32, ints_hi, ints_lo, packed, outbox, inbox, gathered, product, sums_out, sums_in,
    totals, denom_ref, fetch_sem, a_send, a_recv, s_send, s_recv, a_ready, s_ready,
):
    b = lax.axis_index("blk")
    c = lax.axis_index("ctr")
    rank = rank_of(b)
    early = 14
    groups = nb // NIRR
    sources = nb // CHUNKS
    ab, cd = ints_f32.shape
    share = ab // nc
    irreps, mine, _ = amps_ref.shape
    full = cd // LANES
    rest = cd - full * LANES
    ij = nb * mine
    width = ij // CHUNKS
    height = sums_out.shape[2]
    starts = [min(g * height, share - height) for g in range(CHUNKS)]
    fetches = [
        pltpu.make_async_copy(src, dst, fetch_sem.at[i])
        for i, (src, dst) in enumerate(
            [(blockmap_hbm, blockmap_ref), (amps_hbm, amps_ref), (occ_hbm, occ_ref), (vir_hbm, vir_ref.at[0]),
             (ints_hbm, ints_f32)]
        )
    ]
    for fetch in fetches:
        fetch.start()

    barrier = pltpu.get_barrier_semaphore()

    @pl.loop(rank + 1, nb)
    def _(r):
        pl.semaphore_signal(barrier, inc=1, device_id=(at_rank(r), c), device_id_type=MESH)

    @pl.loop(c + 1, nc)
    def _(p):
        pl.semaphore_signal(barrier, inc=1, device_id=(b, p), device_id_type=MESH)

    @pl.when(rank + c > 0)
    def _():
        pl.semaphore_wait(barrier, rank + c)

    for p in range(nb):
        @pl.when(rank_of(jnp.int32(p)) < rank)
        def _():
            pl.semaphore_signal(a_ready.at[b], inc=1, device_id=(p, c), device_id_type=MESH)

    @pl.loop(0, c)
    def _(p):
        pl.semaphore_signal(s_ready, inc=1, device_id=(b, p), device_id_type=MESH)

    fetches[0].wait()
    fetches[1].wait()
    for h in range(irreps):
        for t in range(full):
            packed[h, t * mine:(t + 1) * mine, :] = amps_ref[h, :, t * LANES:(t + 1) * LANES]
        packed[h, full * mine:full * mine + 1, :] = jnp.concatenate(
            [amps_ref[h, u:u + 1, full * LANES:cd] for u in range(mine)], axis=1
        )

    def amps_copy(to):
        return pltpu.make_async_remote_copy(
            src_ref=outbox.at[to], dst_ref=inbox.at[b], send_sem=a_send, recv_sem=a_recv.at[b // sources],
            device_id=(to, c), device_id_type=MESH,
        )

    def visit(to):
        @pl.when(rank_of(to) > rank)
        def _():
            pl.semaphore_wait(a_ready.at[to], 1)

        outbox[to] = packed[blockmap_ref[to] >> 2]
        amps_copy(to).start()

    def far(i):
        return (b + nb // 2 + ((i + 1) >> 1) * (2 * (i & 1) - 1)) & (nb - 1)

    @pl.when(rank < early)
    def _():
        @pl.loop(0, early)
        def _(r):
            @pl.when(r != rank)
            def _():
                visit(at_rank(r))

    @pl.when(rank >= early)
    def _():
        @pl.loop(0, nb - 1)
        def _(i):
            to = far(i)

            @pl.when(rank_of(to) < early)
            def _():
                visit(to)

    @pl.loop(0, nb - 1)
    def _(i):
        to = far(i)

        @pl.when(rank_of(to) >= early)
        def _():
            visit(to)

    outbox[b] = packed[blockmap_ref[b] >> 2]
    pltpu.make_async_copy(outbox.at[b], inbox.at[b], a_recv.at[b // sources]).start()
    fetches[2].wait()
    fetches[3].wait()
    denom_ref[...] = denominator(
        blockmap_ref[b], groups, ab, c * share, share, ij, vir_ref[...], occ_ref
    )
    fetches[4].wait()
    value = ints_f32[...]
    high = value.astype(jnp.bfloat16)
    ints_hi[...] = high
    ints_lo[...] = (value - high.astype(jnp.float32)).astype(jnp.bfloat16)

    def sums_copy(j, to):
        return pltpu.make_async_remote_copy(
            src_ref=sums_out.at[j, to], dst_ref=sums_in.at[j, c],
            send_sem=s_send.at[j], recv_sem=s_recv.at[j],
            device_id=(b, to), device_id_type=MESH,
        )

    lane = lax.broadcasted_iota(jnp.int32, (height, ij), 1)
    dot = functools.partial(lax.dot_general, dimension_numbers=NT, preferred_element_type=jnp.float32)

    def multiply(j):
        base = j * sources

        arrived = inbox.at[pl.ds(base, sources)]
        pltpu.make_async_copy(arrived, arrived, a_recv.at[j]).wait()

        for p in range(sources):
            for t in range(full):
                gathered[p * mine:(p + 1) * mine, t * LANES:(t + 1) * LANES] = (
                    inbox[base + p, t * mine:(t + 1) * mine, :]
                )
            row = inbox[base + p, full * mine:full * mine + 1, :]
            for u in range(mine):
                gathered[p * mine + u:p * mine + u + 1, full * LANES:cd] = row[:, u * rest:(u + 1) * rest]
        amps = gathered[...]
        amps_hi = amps.astype(jnp.bfloat16)
        amps_lo = (amps - amps_hi.astype(jnp.float32)).astype(jnp.bfloat16)
        both = jnp.concatenate([amps_hi] * CHUNKS + [amps_lo] * CHUNKS, axis=0)
        step = 160

        def rows_of(r):
            wide = dot(ints_hi[r:r + step, :], both)
            product[r:r + step, :] = (
                (dot(ints_lo[r:r + step, :], both[:ij]) + wide[:, ij:]) + wide[:, :ij]
            )

        def pack(p):
            rows = [product[p * share + start:p * share + start + height, :] for start in starts]
            block = rows[-1]
            for g in range(CHUNKS - 2, -1, -1):
                block = jnp.where(lane < (g + 1) * width, rows[g], block)
            sums_out[j, p] = block

        done = 0
        for r in range(0, ab, step):
            rows_of(r)
            ready = (r + step) // share
            for p in range(done, ready):
                pack(p)
            for p in range(done, ready):
                @pl.when(p != c)
                def _():
                    sums_copy(j, p).start()
            done = ready

        pltpu.make_async_copy(sums_out.at[j, c], sums_in.at[j, c], s_recv.at[j]).start()

    def add_up(j):
        pltpu.make_async_copy(sums_in.at[j], sums_in.at[j], s_recv.at[j]).wait()
        total = sums_in[j, 0]
        for p in range(1, nc):
            total = total + sums_in[j, p]
        totals[j] = total

    order = [0, 1, 3, 2] if CHUNKS == 4 else list(range(CHUNKS))
    for place, j in enumerate(order):
        multiply_at = j
        if place == 0:
            @pl.when(c < nc - 1)
            def _():
                pl.semaphore_wait(s_ready, nc - 1 - c)
        multiply(multiply_at)
    sent = outbox.at[pl.ds(0, nb - 1)]
    pltpu.make_async_copy(sent, sent, a_send).wait()
    for j in order:
        sent = sums_out.at[j, pl.ds(0, nc - 1)]
        pltpu.make_async_copy(sent, sent, s_send.at[j]).wait()
    for j in order:
        add_up(j)

    for g, start in enumerate(starts):
        block = None
        for j in range(CHUNKS):
            turned = totals[j]
            if (j - g) % CHUNKS:
                turned = pltpu.roll(turned, (j - g) % CHUNKS * width, 1)
            block = turned if block is None else jnp.where(lane < j * width, block, turned)
        ladder_ref[start:start + height, 0, :] = block
        incr_ref[start:start + height, 0, :] = block / denom_ref[start:start + height, :]


def on_device(integrals, amplitudes, blockmap, vir_energy, occ_energy):
    nb, nc = lax.axis_size("blk"), lax.axis_size("ctr")
    _, ab, cd = integrals.shape
    irreps, _, mine = amplitudes.shape
    ij = mine * nb
    share = ab // nc
    height = -(-share // CHUNKS)
    rows = mine * cd // LANES
    vmem = pl.BlockSpec(memory_space=pltpu.VMEM)
    hbm = pl.BlockSpec(memory_space=pltpu.HBM)
    out = jax.ShapeDtypeStruct((share, 1, ij), jnp.float32)
    ladder, increment = pl.pallas_call(
        functools.partial(kernel, nb, nc),
        out_shape=(out, out),
        in_specs=[hbm] * 5,
        out_specs=(vmem, vmem),
        scratch_shapes=[
            pltpu.SMEM(blockmap.shape, jnp.int32),
            pltpu.SMEM(occ_energy.shape, jnp.float32),
            pltpu.VMEM((1, vir_energy.shape[0]), jnp.float32),
            pltpu.VMEM((irreps, mine, cd), jnp.float32),
            pltpu.VMEM((ab, cd), jnp.float32),
            pltpu.VMEM((ab, cd), jnp.bfloat16),
            pltpu.VMEM((ab, cd), jnp.bfloat16),
            pltpu.VMEM((irreps, rows, LANES), jnp.float32),
            pltpu.VMEM((nb, rows, LANES), jnp.float32),
            pltpu.VMEM((nb, rows, LANES), jnp.float32),
            pltpu.VMEM((ij // CHUNKS, cd), jnp.float32),
            pltpu.VMEM((ab, ij), jnp.float32),
            pltpu.VMEM((CHUNKS, nc, height, ij), jnp.float32),
            pltpu.VMEM((CHUNKS, nc, height, ij), jnp.float32),
            pltpu.VMEM((CHUNKS, height, ij), jnp.float32),
            pltpu.VMEM((share, ij), jnp.float32),
            pltpu.SemaphoreType.DMA((5,)),
            pltpu.SemaphoreType.DMA,
            pltpu.SemaphoreType.DMA((CHUNKS,)),
            pltpu.SemaphoreType.DMA((CHUNKS,)),
            pltpu.SemaphoreType.DMA((CHUNKS,)),
            pltpu.SemaphoreType.REGULAR((nb,)),
            pltpu.SemaphoreType.REGULAR,
        ],
        compiler_params=pltpu.CompilerParams(
            collective_id=0, has_side_effects=True, vmem_limit_bytes=VLIM
        ),
    )(
        *(
            pltpu.with_memory_space_constraint(x, pltpu.HBM)
            for x in (blockmap, occ_energy, vir_energy, jnp.transpose(amplitudes, (0, 2, 1)), integrals[0])
        )
    )
    return jnp.transpose(ladder, (1, 0, 2)), jnp.transpose(increment, (1, 0, 2))


def solution(mesh):
    placed = (P("blk", None, "ctr"), P(None, "ctr", "blk"), P(), P(), P())
    return jax.shard_map(
        on_device,
        mesh=mesh,
        in_specs=placed,
        out_specs=(P("blk", "ctr", None), P("blk", "ctr", None)),
        check_vma=False,
    )
```

```python
import functools

import jax
import jax.numpy as jnp
from jax import lax
from jax.experimental import pallas as pl
from jax.experimental.pallas import tpu as pltpu
from jax.sharding import PartitionSpec as P

NIRR = 8
VI = 40
OI = 4
LANES = 128
MESH = pl.DeviceIdType.MESH
CHUNKS = 2
VLIM = 52 << 20
NT = (((1,), (1,)), ((), ()))


def denominator(block, groups, ab_block, start, count, columns, vir, occ_ref):
    irrep = block >> 2
    quarter = block - irrep * groups
    rows = quarter * ab_block + start + lax.broadcasted_iota(jnp.int32, (count, 1), 0)
    first = (rows * 52429) >> 21
    digit = rows - first * VI
    arow = (first * 52429) >> 21
    second = jnp.bitwise_xor(arow, irrep) * VI + digit
    index = lax.broadcasted_iota(jnp.int32, (1, vir.shape[1]), 1)
    up_one = jnp.sum(jnp.where(index == first, vir, 0.0), axis=1, keepdims=True)
    up_two = jnp.sum(jnp.where(index == second, vir, 0.0), axis=1, keepdims=True)
    cols = lax.broadcasted_iota(jnp.int32, (1, columns), 1)
    hole_one = cols >> 2
    hole_two = jnp.bitwise_xor(cols >> 4, irrep) * OI + (cols & 3)
    low_one = jnp.zeros((1, columns), jnp.float32)
    low_two = jnp.zeros((1, columns), jnp.float32)
    for o in range(NIRR * OI):
        low_one = jnp.where(hole_one == o, occ_ref[o], low_one)
        low_two = jnp.where(hole_two == o, occ_ref[o], low_two)
    return (up_one + up_two) - (low_one + low_two)


def rank_of(b):
    z = b >> 1
    return 2 * jnp.where(z < 7, z, jnp.where(z < 11, 2 * z - 6, 37 - 2 * z)) + (b & 1)


def at_rank(rank):
    place = rank >> 1
    half = (place - 7) >> 1
    z = jnp.where(place < 7, place, jnp.where((place & 1) == 1, 15 - half, 7 + half))
    return 2 * z + (rank & 1)


def kernel(
    nb, nc, blockmap_hbm, occ_hbm, vir_hbm, amps_hbm, ints_hbm,
    half_one_ref, half_two_ref, denom_ref,
    blockmap_ref, occ_ref, vir_ref, amps_ref,
    ints_f32, ints_hi, ints_lo, packed, outbox, inbox, gathered, product, sums_out, sums_in,
    totals, fetch_sem, a_send, a_recv, s_send, s_recv, a_ready, s_ready,
):
    b = lax.axis_index("blk")
    c = lax.axis_index("ctr")
    rank = rank_of(b)
    early = 14
    groups = nb // NIRR
    sources = nb // CHUNKS
    ab, cd = ints_f32.shape
    share = ab // nc
    irreps, mine, _ = amps_ref.shape
    full = cd // LANES
    rest = cd - full * LANES
    ij = nb * mine
    width = ij // CHUNKS
    height = sums_out.shape[2]
    starts = [min(g * height, share - height) for g in range(CHUNKS)]
    fetches = [
        pltpu.make_async_copy(src, dst, fetch_sem.at[i])
        for i, (src, dst) in enumerate(
            [(blockmap_hbm, blockmap_ref), (amps_hbm, amps_ref), (occ_hbm, occ_ref), (vir_hbm, vir_ref.at[0]),
             (ints_hbm, ints_f32)]
        )
    ]
    for fetch in fetches:
        fetch.start()

    barrier = pltpu.get_barrier_semaphore()

    @pl.loop(rank + 1, nb)
    def _(r):
        pl.semaphore_signal(barrier, inc=1, device_id=(at_rank(r), c), device_id_type=MESH)

    @pl.loop(c + 1, nc)
    def _(p):
        pl.semaphore_signal(barrier, inc=1, device_id=(b, p), device_id_type=MESH)

    @pl.when(rank + c > 0)
    def _():
        pl.semaphore_wait(barrier, rank + c)

    for p in range(nb):
        @pl.when(rank_of(jnp.int32(p)) < rank)
        def _():
            pl.semaphore_signal(a_ready.at[b], inc=1, device_id=(p, c), device_id_type=MESH)

    @pl.loop(0, c)
    def _(p):
        pl.semaphore_signal(s_ready, inc=1, device_id=(b, p), device_id_type=MESH)

    fetches[0].wait()
    fetches[1].wait()
    for h in range(irreps):
        for t in range(full):
            packed[h, t * mine:(t + 1) * mine, :] = amps_ref[h, :, t * LANES:(t + 1) * LANES]
        packed[h, full * mine:full * mine + 1, :] = jnp.concatenate(
            [amps_ref[h, u:u + 1, full * LANES:cd] for u in range(mine)], axis=1
        )

    def amps_copy(to):
        return pltpu.make_async_remote_copy(
            src_ref=outbox.at[to], dst_ref=inbox.at[b], send_sem=a_send, recv_sem=a_recv.at[b // sources],
            device_id=(to, c), device_id_type=MESH,
        )

    def visit(to):
        @pl.when(rank_of(to) > rank)
        def _():
            pl.semaphore_wait(a_ready.at[to], 1)

        outbox[to] = packed[blockmap_ref[to] >> 2]
        amps_copy(to).start()

    def far(i):
        return (b + nb // 2 + ((i + 1) >> 1) * (2 * (i & 1) - 1)) & (nb - 1)

    @pl.when(rank < early)
    def _():
        @pl.loop(0, early)
        def _(r):
            @pl.when(r != rank)
            def _():
                visit(at_rank(r))

    @pl.when(rank >= early)
    def _():
        @pl.loop(0, nb - 1)
        def _(i):
            to = far(i)

            @pl.when(rank_of(to) < early)
            def _():
                visit(to)

    @pl.loop(0, nb - 1)
    def _(i):
        to = far(i)

        @pl.when(rank_of(to) >= early)
        def _():
            visit(to)

    outbox[b] = packed[blockmap_ref[b] >> 2]
    pltpu.make_async_copy(outbox.at[b], inbox.at[b], a_recv.at[b // sources]).start()
    fetches[2].wait()
    fetches[3].wait()
    denom_ref[:, 0, :] = denominator(
        blockmap_ref[b], groups, ab, c * share, share, ij, vir_ref[...], occ_ref
    )
    fetches[4].wait()
    value = ints_f32[...]
    high = value.astype(jnp.bfloat16)
    ints_hi[...] = high
    ints_lo[...] = (value - high.astype(jnp.float32)).astype(jnp.bfloat16)

    def sums_copy(j, to):
        return pltpu.make_async_remote_copy(
            src_ref=sums_out.at[j, to], dst_ref=sums_in.at[j, c],
            send_sem=s_send.at[j], recv_sem=s_recv.at[j],
            device_id=(b, to), device_id_type=MESH,
        )

    lane = lax.broadcasted_iota(jnp.int32, (height, ij), 1)
    dot = functools.partial(lax.dot_general, dimension_numbers=NT, preferred_element_type=jnp.float32)

    def multiply(j):
        base = j * sources

        arrived = inbox.at[pl.ds(base, sources)]
        pltpu.make_async_copy(arrived, arrived, a_recv.at[j]).wait()

        for p in range(sources):
            for t in range(full):
                gathered[p * mine:(p + 1) * mine, t * LANES:(t + 1) * LANES] = (
                    inbox[base + p, t * mine:(t + 1) * mine, :]
                )
            row = inbox[base + p, full * mine:full * mine + 1, :]
            for u in range(mine):
                gathered[p * mine + u:p * mine + u + 1, full * LANES:cd] = row[:, u * rest:(u + 1) * rest]
        amps = gathered[...]
        amps_hi = amps.astype(jnp.bfloat16)
        amps_lo = (amps - amps_hi.astype(jnp.float32)).astype(jnp.bfloat16)
        both = jnp.concatenate([amps_hi] * CHUNKS + [amps_lo] * CHUNKS, axis=0)
        step = 160

        def rows_of(r):
            wide = dot(ints_hi[r:r + step, :], both)
            product[r:r + step, :] = (
                (dot(ints_lo[r:r + step, :], both[:ij]) + wide[:, ij:]) + wide[:, :ij]
            )

        def pack(p):
            rows = [product[p * share + start:p * share + start + height, :] for start in starts]
            block = rows[-1]
            for g in range(CHUNKS - 2, -1, -1):
                block = jnp.where(lane < (g + 1) * width, rows[g], block)
            sums_out[j, p] = block

        done = 0
        for r in range(0, ab, step):
            rows_of(r)
            ready = (r + step) // share
            for p in range(done, ready):
                pack(p)
            for p in range(done, ready):
                @pl.when(p != c)
                def _():
                    sums_copy(j, p).start()
            done = ready

        pltpu.make_async_copy(sums_out.at[j, c], sums_in.at[j, c], s_recv.at[j]).start()

    def add_up(j):
        pltpu.make_async_copy(sums_in.at[j], sums_in.at[j], s_recv.at[j]).wait()
        for half in range(2):
            total = sums_in[j, half * nc // 2]
            for p in range(half * nc // 2 + 1, (half + 1) * nc // 2):
                total = total + sums_in[j, p]
            totals[half, j] = total

    order = [0, 1, 3, 2] if CHUNKS == 4 else list(range(CHUNKS))
    for place, j in enumerate(order):
        multiply_at = j
        if place == 0:
            @pl.when(c < nc - 1)
            def _():
                pl.semaphore_wait(s_ready, nc - 1 - c)
        multiply(multiply_at)
    sent = outbox.at[pl.ds(0, nb - 1)]
    pltpu.make_async_copy(sent, sent, a_send).wait()
    for j in order:
        sent = sums_out.at[j, pl.ds(0, nc - 1)]
        pltpu.make_async_copy(sent, sent, s_send.at[j]).wait()
    for j in order:
        add_up(j)

    for half, half_ref in enumerate([half_one_ref, half_two_ref]):
        for g, start in enumerate(starts):
            block = None
            for j in range(CHUNKS):
                turned = totals[half, j]
                if (j - g) % CHUNKS:
                    turned = pltpu.roll(turned, (j - g) % CHUNKS * width, 1)
                block = turned if block is None else jnp.where(lane < j * width, block, turned)
            half_ref[start:start + height, 0, :] = block


def on_device(integrals, amplitudes, blockmap, vir_energy, occ_energy):
    nb, nc = lax.axis_size("blk"), lax.axis_size("ctr")
    _, ab, cd = integrals.shape
    irreps, _, mine = amplitudes.shape
    ij = mine * nb
    share = ab // nc
    height = -(-share // CHUNKS)
    rows = mine * cd // LANES
    vmem = pl.BlockSpec(memory_space=pltpu.VMEM)
    hbm = pl.BlockSpec(memory_space=pltpu.HBM)
    out = jax.ShapeDtypeStruct((share, 1, ij), jnp.float32)
    half_one, half_two, denom = pl.pallas_call(
        functools.partial(kernel, nb, nc),
        out_shape=(out, out, out),
        in_specs=[hbm] * 5,
        out_specs=(vmem, vmem, vmem),
        scratch_shapes=[
            pltpu.SMEM(blockmap.shape, jnp.int32),
            pltpu.SMEM(occ_energy.shape, jnp.float32),
            pltpu.VMEM((1, vir_energy.shape[0]), jnp.float32),
            pltpu.VMEM((irreps, mine, cd), jnp.float32),
            pltpu.VMEM((ab, cd), jnp.float32),
            pltpu.VMEM((ab, cd), jnp.bfloat16),
            pltpu.VMEM((ab, cd), jnp.bfloat16),
            pltpu.VMEM((irreps, rows, LANES), jnp.float32),
            pltpu.VMEM((nb, rows, LANES), jnp.float32),
            pltpu.VMEM((nb, rows, LANES), jnp.float32),
            pltpu.VMEM((ij // CHUNKS, cd), jnp.float32),
            pltpu.VMEM((ab, ij), jnp.float32),
            pltpu.VMEM((CHUNKS, nc, height, ij), jnp.float32),
            pltpu.VMEM((CHUNKS, nc, height, ij), jnp.float32),
            pltpu.VMEM((2, CHUNKS, height, ij), jnp.float32),
            pltpu.SemaphoreType.DMA((5,)),
            pltpu.SemaphoreType.DMA,
            pltpu.SemaphoreType.DMA((CHUNKS,)),
            pltpu.SemaphoreType.DMA((CHUNKS,)),
            pltpu.SemaphoreType.DMA((CHUNKS,)),
            pltpu.SemaphoreType.REGULAR((nb,)),
            pltpu.SemaphoreType.REGULAR,
        ],
        compiler_params=pltpu.CompilerParams(
            collective_id=0, has_side_effects=True, vmem_limit_bytes=VLIM
        ),
    )(
        *(
            pltpu.with_memory_space_constraint(x, pltpu.HBM)
            for x in (blockmap, occ_energy, vir_energy, jnp.transpose(amplitudes, (0, 2, 1)), integrals[0])
        )
    )
    ladder = half_one + half_two
    return jnp.transpose(ladder, (1, 0, 2)), jnp.transpose(ladder / denom, (1, 0, 2))


def solution(mesh):
    placed = (P("blk", None, "ctr"), P(None, "ctr", "blk"), P(), P(), P())
    return jax.shard_map(
        on_device,
        mesh=mesh,
        in_specs=placed,
        out_specs=(P("blk", "ctr", None), P("blk", "ctr", None)),
        check_vma=False,
    )
```

```python
import functools

import jax
import jax.numpy as jnp
from jax import lax
from jax.experimental import pallas as pl
from jax.experimental.pallas import tpu as pltpu
from jax.sharding import PartitionSpec as P

NIRR = 8
VI = 40
OI = 4
LANES = 128
MESH = pl.DeviceIdType.MESH
CHUNKS = 2
VLIM = 52 << 20
NT = (((1,), (1,)), ((), ()))


def denominator(block, groups, ab_block, start, count, columns, vir, occ_ref):
    irrep = block >> 2
    quarter = block - irrep * groups
    rows = quarter * ab_block + start + lax.broadcasted_iota(jnp.int32, (count, 1), 0)
    first = (rows * 52429) >> 21
    digit = rows - first * VI
    arow = (first * 52429) >> 21
    second = jnp.bitwise_xor(arow, irrep) * VI + digit
    index = lax.broadcasted_iota(jnp.int32, (1, vir.shape[1]), 1)
    up_one = jnp.sum(jnp.where(index == first, vir, 0.0), axis=1, keepdims=True)
    up_two = jnp.sum(jnp.where(index == second, vir, 0.0), axis=1, keepdims=True)
    cols = lax.broadcasted_iota(jnp.int32, (1, columns), 1)
    hole_one = cols >> 2
    hole_two = jnp.bitwise_xor(cols >> 4, irrep) * OI + (cols & 3)
    low_one = jnp.zeros((1, columns), jnp.float32)
    low_two = jnp.zeros((1, columns), jnp.float32)
    for o in range(NIRR * OI):
        low_one = jnp.where(hole_one == o, occ_ref[o], low_one)
        low_two = jnp.where(hole_two == o, occ_ref[o], low_two)
    return (up_one + up_two) - (low_one + low_two)


def rank_of(b):
    z = b >> 1
    return 2 * jnp.where(z < 7, z, jnp.where(z < 11, 2 * z - 6, 37 - 2 * z)) + (b & 1)


def at_rank(rank):
    place = rank >> 1
    half = (place - 7) >> 1
    z = jnp.where(place < 7, place, jnp.where((place & 1) == 1, 15 - half, 7 + half))
    return 2 * z + (rank & 1)


def kernel(
    nb, nc, blockmap_hbm, occ_hbm, vir_hbm, amps_hbm, ints_hbm,
    half_one_ref, half_two_ref, denom_ref,
    blockmap_ref, occ_ref, vir_ref, amps_ref,
    ints_f32, ints_hi, ints_lo, packed, outbox, inbox, gathered, product, sums_out, sums_in,
    totals, fetch_sem, a_send, a_recv, s_send, s_recv, a_ready, s_ready,
):
    b = lax.axis_index("blk")
    c = lax.axis_index("ctr")
    rank = rank_of(b)
    early = 15
    groups = nb // NIRR
    sources = nb // CHUNKS
    ab, cd = ints_f32.shape
    share = ab // nc
    irreps, mine, _ = amps_ref.shape
    full = cd // LANES
    rest = cd - full * LANES
    ij = nb * mine
    width = ij // CHUNKS
    height = sums_out.shape[2]
    starts = [min(g * height, share - height) for g in range(CHUNKS)]
    fetches = [
        pltpu.make_async_copy(src, dst, fetch_sem.at[i])
        for i, (src, dst) in enumerate(
            [(blockmap_hbm, blockmap_ref), (amps_hbm, amps_ref), (occ_hbm, occ_ref), (vir_hbm, vir_ref.at[0]),
             (ints_hbm, ints_f32)]
        )
    ]
    for fetch in fetches:
        fetch.start()

    barrier = pltpu.get_barrier_semaphore()

    @pl.loop(rank + 1, nb)
    def _(r):
        pl.semaphore_signal(barrier, inc=1, device_id=(at_rank(r), c), device_id_type=MESH)

    @pl.loop(c + 1, nc)
    def _(p):
        pl.semaphore_signal(barrier, inc=1, device_id=(b, p), device_id_type=MESH)

    @pl.when(rank + c > 0)
    def _():
        pl.semaphore_wait(barrier, rank + c)

    for p in range(nb):
        @pl.when(rank_of(jnp.int32(p)) < rank)
        def _():
            pl.semaphore_signal(a_ready.at[b], inc=1, device_id=(p, c), device_id_type=MESH)

    @pl.loop(0, c)
    def _(p):
        pl.semaphore_signal(s_ready, inc=1, device_id=(b, p), device_id_type=MESH)

    fetches[0].wait()
    fetches[1].wait()
    for h in range(irreps):
        for t in range(full):
            packed[h, t * mine:(t + 1) * mine, :] = amps_ref[h, :, t * LANES:(t + 1) * LANES]
        packed[h, full * mine:full * mine + 1, :] = jnp.concatenate(
            [amps_ref[h, u:u + 1, full * LANES:cd] for u in range(mine)], axis=1
        )

    def amps_copy(to):
        return pltpu.make_async_remote_copy(
            src_ref=outbox.at[to], dst_ref=inbox.at[b], send_sem=a_send, recv_sem=a_recv.at[b // sources],
            device_id=(to, c), device_id_type=MESH,
        )

    def visit(to):
        @pl.when(rank_of(to) > rank)
        def _():
            pl.semaphore_wait(a_ready.at[to], 1)

        outbox[to] = packed[blockmap_ref[to] >> 2]
        amps_copy(to).start()

    def far(i):
        return (b + nb // 2 + ((i + 1) >> 1) * (2 * (i & 1) - 1)) & (nb - 1)

    @pl.when(rank < early)
    def _():
        @pl.loop(0, early)
        def _(r):
            @pl.when(r != rank)
            def _():
                visit(at_rank(r))

    @pl.when(rank >= early)
    def _():
        @pl.loop(0, nb - 1)
        def _(i):
            to = far(i)

            @pl.when(rank_of(to) < early)
            def _():
                visit(to)

    @pl.loop(0, nb - 1)
    def _(i):
        to = far(i)

        @pl.when(rank_of(to) >= early)
        def _():
            visit(to)

    outbox[b] = packed[blockmap_ref[b] >> 2]
    pltpu.make_async_copy(outbox.at[b], inbox.at[b], a_recv.at[b // sources]).start()
    fetches[2].wait()
    fetches[3].wait()
    denom_ref[:, 0, :] = denominator(
        blockmap_ref[b], groups, ab, c * share, share, ij, vir_ref[...], occ_ref
    )
    fetches[4].wait()
    value = ints_f32[...]
    high = value.astype(jnp.bfloat16)
    ints_hi[...] = high
    ints_lo[...] = (value - high.astype(jnp.float32)).astype(jnp.bfloat16)

    def sums_copy(j, to):
        return pltpu.make_async_remote_copy(
            src_ref=sums_out.at[j, to], dst_ref=sums_in.at[j, c],
            send_sem=s_send.at[j], recv_sem=s_recv.at[j],
            device_id=(b, to), device_id_type=MESH,
        )

    lane = lax.broadcasted_iota(jnp.int32, (height, ij), 1)
    dot = functools.partial(lax.dot_general, dimension_numbers=NT, preferred_element_type=jnp.float32)

    def multiply(j):
        base = j * sources

        arrived = inbox.at[pl.ds(base, sources)]
        pltpu.make_async_copy(arrived, arrived, a_recv.at[j]).wait()

        for p in range(sources):
            for t in range(full):
                gathered[p * mine:(p + 1) * mine, t * LANES:(t + 1) * LANES] = (
                    inbox[base + p, t * mine:(t + 1) * mine, :]
                )
            row = inbox[base + p, full * mine:full * mine + 1, :]
            for u in range(mine):
                gathered[p * mine + u:p * mine + u + 1, full * LANES:cd] = row[:, u * rest:(u + 1) * rest]
        amps = gathered[...]
        amps_hi = amps.astype(jnp.bfloat16)
        amps_lo = (amps - amps_hi.astype(jnp.float32)).astype(jnp.bfloat16)
        both = jnp.concatenate([amps_hi] * CHUNKS + [amps_lo] * CHUNKS, axis=0)
        step = 160

        def rows_of(r):
            wide = dot(ints_hi[r:r + step, :], both)
            product[r:r + step, :] = (
                (dot(ints_lo[r:r + step, :], both[:ij]) + wide[:, ij:]) + wide[:, :ij]
            )

        def pack(p):
            rows = [product[p * share + start:p * share + start + height, :] for start in starts]
            block = rows[-1]
            for g in range(CHUNKS - 2, -1, -1):
                block = jnp.where(lane < (g + 1) * width, rows[g], block)
            sums_out[j, p] = block

        done = 0
        for r in range(0, ab, step):
            rows_of(r)
            ready = (r + step) // share
            for p in range(done, ready):
                pack(p)
            for p in range(done, ready):
                @pl.when(p != c)
                def _():
                    sums_copy(j, p).start()
            done = ready

        pltpu.make_async_copy(sums_out.at[j, c], sums_in.at[j, c], s_recv.at[j]).start()

    def add_up(j):
        pltpu.make_async_copy(sums_in.at[j], sums_in.at[j], s_recv.at[j]).wait()
        for half in range(2):
            total = sums_in[j, half * nc // 2]
            for p in range(half * nc // 2 + 1, (half + 1) * nc // 2):
                total = total + sums_in[j, p]
            totals[half, j] = total

    order = [0, 1, 3, 2] if CHUNKS == 4 else list(range(CHUNKS))
    for place, j in enumerate(order):
        multiply_at = j
        if place == 0:
            @pl.when(c < nc - 1)
            def _():
                pl.semaphore_wait(s_ready, nc - 1 - c)
        multiply(multiply_at)
    for j in order[:-1]:
        add_up(j)
    sent = outbox.at[pl.ds(0, nb - 1)]
    pltpu.make_async_copy(sent, sent, a_send).wait()
    for j in order:
        sent = sums_out.at[j, pl.ds(0, nc - 1)]
        pltpu.make_async_copy(sent, sent, s_send.at[j]).wait()
    add_up(order[-1])

    for half, half_ref in enumerate([half_one_ref, half_two_ref]):
        for g, start in enumerate(starts):
            block = None
            for j in range(CHUNKS):
                turned = totals[half, j]
                if (j - g) % CHUNKS:
                    turned = pltpu.roll(turned, (j - g) % CHUNKS * width, 1)
                block = turned if block is None else jnp.where(lane < j * width, block, turned)
            half_ref[start:start + height, 0, :] = block


def on_device(integrals, amplitudes, blockmap, vir_energy, occ_energy):
    nb, nc = lax.axis_size("blk"), lax.axis_size("ctr")
    _, ab, cd = integrals.shape
    irreps, _, mine = amplitudes.shape
    ij = mine * nb
    share = ab // nc
    height = -(-share // CHUNKS)
    rows = mine * cd // LANES
    vmem = pl.BlockSpec(memory_space=pltpu.VMEM)
    hbm = pl.BlockSpec(memory_space=pltpu.HBM)
    out = jax.ShapeDtypeStruct((share, 1, ij), jnp.float32)
    half_one, half_two, denom = pl.pallas_call(
        functools.partial(kernel, nb, nc),
        out_shape=(out, out, out),
        in_specs=[hbm] * 5,
        out_specs=(vmem, vmem, vmem),
        scratch_shapes=[
            pltpu.SMEM(blockmap.shape, jnp.int32),
            pltpu.SMEM(occ_energy.shape, jnp.float32),
            pltpu.VMEM((1, vir_energy.shape[0]), jnp.float32),
            pltpu.VMEM((irreps, mine, cd), jnp.float32),
            pltpu.VMEM((ab, cd), jnp.float32),
            pltpu.VMEM((ab, cd), jnp.bfloat16),
            pltpu.VMEM((ab, cd), jnp.bfloat16),
            pltpu.VMEM((irreps, rows, LANES), jnp.float32),
            pltpu.VMEM((nb, rows, LANES), jnp.float32),
            pltpu.VMEM((nb, rows, LANES), jnp.float32),
            pltpu.VMEM((ij // CHUNKS, cd), jnp.float32),
            pltpu.VMEM((ab, ij), jnp.float32),
            pltpu.VMEM((CHUNKS, nc, height, ij), jnp.float32),
            pltpu.VMEM((CHUNKS, nc, height, ij), jnp.float32),
            pltpu.VMEM((2, CHUNKS, height, ij), jnp.float32),
            pltpu.SemaphoreType.DMA((5,)),
            pltpu.SemaphoreType.DMA,
            pltpu.SemaphoreType.DMA((CHUNKS,)),
            pltpu.SemaphoreType.DMA((CHUNKS,)),
            pltpu.SemaphoreType.DMA((CHUNKS,)),
            pltpu.SemaphoreType.REGULAR((nb,)),
            pltpu.SemaphoreType.REGULAR,
        ],
        compiler_params=pltpu.CompilerParams(
            collective_id=0, has_side_effects=True, vmem_limit_bytes=VLIM
        ),
    )(
        *(
            pltpu.with_memory_space_constraint(x, pltpu.HBM)
            for x in (blockmap, occ_energy, vir_energy, jnp.transpose(amplitudes, (0, 2, 1)), integrals[0])
        )
    )
    ladder = half_one + half_two
    return jnp.transpose(ladder, (1, 0, 2)), jnp.transpose(ladder / denom, (1, 0, 2))


def solution(mesh):
    placed = (P("blk", None, "ctr"), P(None, "ctr", "blk"), P(), P(), P())
    return jax.shard_map(
        on_device,
        mesh=mesh,
        in_specs=placed,
        out_specs=(P("blk", "ctr", None), P("blk", "ctr", None)),
        check_vma=False,
    )
```
